768 devices in a mesh: seq: 64 (over y, x, core), head: 12 (over z).
Axes of the slice: x: 4, y: 8, z: 12, core: 2. Of those that a mesh axis runs over, the one named last changes fastest.
Arguments:
- qkv: bfloat16 [98304, 4096], P(('seq', 'head')), may hold values from -24 to 24
- residual: bfloat16 [98304, 2048], P(('seq', 'head')), may hold values from -1.5 to 1.5
- dest_row: int32 [98304], P(('seq', 'head')), may hold values from 0 to 98303, as said below
- source_row: int32 [98304], P(('seq', 'head')), may hold values from 0 to 98303, as said below
- doc_start: int32 [98304], P('seq'), may hold values from 0 to 1535, as said below
- out_weight: bfloat16 [3072, 2048], P('head'), may hold values from -0.109375 to 0.109375
- norm_gain: float32 [2048], replicated, may hold values from 0.5 to 1.5
Outputs:
- new_residual: bfloat16 [98304, 2048], P(('seq', 'head'))
- normed: bfloat16 [98304, 2048], P(('seq', 'head'))
The draws below stay inside these ranges and needn't reach their ends.
Inputs may be any that keep to these rules, and one draw needn't show every extreme that they name: `dest_row`: A permutation of all rows. Row (s * 12 + h) * 128 + r goes to a place (g * 12 + h) * 128 + p with the same h. Of the 128 rows of one device, at most 3 go to one group g, every device sends exactly 3 rows to at least one group, and every device receives exactly 3 rows from at least one sender. `source_row`: the inverse permutation of dest_row. Documents are runs of consecutive rows inside one group: doc_start of a row is at most its own group-local index and equals that of the previous row unless the row begins a document; the first row of a group begins a document.
All inputs are finite; a program needn't handle non-finite values.
Results may differ from the reference program's by a relative error of at most 0.014.
Values may be sent and summed in bfloat16 or wider, within the bound.
No kernel may reach another device: no remote copies, remote signals or barrier semaphores. Data moves between devices by JAX's collectives and lax.ppermute only.
A program may use at most 64 MiB of HBM per device.

```python
import jax
import jax.numpy as jnp
from jax import lax

D = 2048
QH = 24
KVH = 4
HD = 128
TOK_DEV = 128
CAP = 3
GROUP = 1536
TOKENS = 98304
QKV = 4096
N_SEQ = 64
N_HEAD = 12


def regroup_tables(key):
    base = jax.random.fold_in(key, 11)
    senders = N_SEQ
    places = N_SEQ * TOK_DEV

    def column(colkey, headidx):
        keys = jax.random.split(colkey, 5)
        chosen = jax.random.permutation(keys[0], (senders - 1) * CAP)[:TOK_DEV - CAP]
        counts = jnp.zeros((senders,), jnp.int32).at[chosen // CAP + 1].add(1)
        counts = counts + jnp.where(jnp.arange(senders) == 0, CAP, 0).astype(jnp.int32)
        bounds = jnp.cumsum(counts)
        binof = jnp.sum((jnp.arange(TOK_DEV)[:, None] >= bounds[None, :]).astype(jnp.int32), axis=1)
        sigma = jax.random.permutation(keys[1], senders)
        tau = jax.random.permutation(keys[2], senders)
        rowperm = jax.vmap(lambda k: jax.random.permutation(k, TOK_DEV))(jax.random.split(keys[3], senders))
        bins = binof[rowperm]
        target = sigma[(tau[:, None] + bins) % senders]
        flat = target.reshape(-1)
        noise = jax.random.permutation(keys[4], places)
        order = jnp.argsort(flat * places + noise, stable=True)
        ranks = jnp.arange(places, dtype=jnp.int32)
        dest_sorted = (ranks // TOK_DEV * N_HEAD + headidx) * TOK_DEV + ranks % TOK_DEV
        dest_flat = jnp.zeros((places,), jnp.int32).at[order].set(dest_sorted.astype(jnp.int32))
        return dest_flat.reshape(senders, TOK_DEV)
    columns = jax.vmap(column)(jax.random.split(base, N_HEAD), jnp.arange(N_HEAD, dtype=jnp.int32))
    dest = jnp.transpose(columns, (1, 0, 2)).reshape(-1).astype(jnp.int32)
    source = jnp.zeros((TOKENS,), jnp.int32).at[dest].set(jnp.arange(TOKENS, dtype=jnp.int32))
    return (dest, source)


def draw_dest_row(key, part):
    return regroup_tables(key)[0]


def draw_source_row(key, part):
    return regroup_tables(key)[1]


def draw_doc_start(key, part):
    first, second = jax.random.split(jax.random.fold_in(key, 7))
    levels = max(1, (GROUP // 8).bit_length())
    exponent = jax.random.randint(first, (N_SEQ, 1), 0, levels)
    spacing = jnp.left_shift(jnp.int32(8), exponent.astype(jnp.int32))
    raw = jax.random.randint(second, (N_SEQ, GROUP), 0, 1 << 20)
    places = jnp.arange(GROUP, dtype=jnp.int32)
    begins = (raw % spacing == 0) | (places[None, :] == 0)
    marker = jnp.where(begins, places[None, :], 0).astype(jnp.int32)
    return lax.cummax(marker, axis=1).reshape(-1).astype(jnp.int32)


def draw_qkv(key, part):
    keys = jax.random.split(jax.random.fold_in(key, 3), 1)
    whole = jnp.clip(jax.random.normal(keys[0], (TOKENS, QKV), jnp.float32), -6.0, 6.0)
    return whole.astype(jnp.bfloat16)


def block_scale(key, shape, cuts, low, high):
    gain, own = 1.0, jax.random.fold_in(key, 6)
    for axis_at, shards_of in cuts:
        heights = jnp.exp(jax.random.uniform(jax.random.fold_in(own, axis_at), (shards_of,), jnp.float32, low / len(cuts), high / len(cuts)))
        gain = gain * jnp.repeat(heights, shape[axis_at] // shards_of).reshape([-1 if axis == axis_at else 1 for axis in range(len(shape))])
    return gain


def scatter_about(key, shape, deviation, limit, cuts=(), kind=jnp.bfloat16):
    level = block_scale(key, shape, cuts, -0.22, 0.18) if cuts else 1.0
    values = jax.random.normal(key, shape, jnp.float32) * deviation * level
    return jnp.minimum(jnp.maximum(values, -limit), limit).astype(kind)


def setup_inputs(seed: int = 0) -> dict:
    streams_of = jax.random.split(jax.random.key(seed), 8)
    return {
        "qkv": draw_qkv(jax.random.fold_in(streams_of[7], 71), 0),
        "residual": scatter_about(streams_of[1], (TOKENS, D), 0.25, 1.5, ((0, 768),)),
        "dest_row": draw_dest_row(jax.random.fold_in(streams_of[7], 71), 0),
        "source_row": draw_source_row(jax.random.fold_in(streams_of[7], 71), 0),
        "doc_start": draw_doc_start(jax.random.fold_in(streams_of[7], 71), 0),
        "out_weight": scatter_about(streams_of[5], (QH * HD, D), (QH * HD) ** -0.5, 0.109375, ((0, 12),)),
        "norm_gain": jnp.clip(1.0 + 0.1 * jax.random.normal(streams_of[6], (D,), jnp.float32), 0.5, 1.5),
    }


def reference(qkv, residual, dest_row, source_row, doc_start, out_weight, norm_gain):
    group_rows = TOK_DEV * N_HEAD
    shared = QH // KVH
    qwidth = QH * HD
    kwidth = KVH * HD
    ordered = qkv[source_row]
    blocks = ordered.reshape(N_SEQ, group_rows, qwidth + 2 * kwidth)
    starts = doc_start.reshape(N_SEQ, group_rows)

    def attend(item):
        rows, first = item
        query = rows[:, :qwidth].reshape(group_rows, QH, HD).astype(jnp.float32)
        keys = rows[:, qwidth:qwidth + kwidth].reshape(group_rows, KVH, HD).astype(jnp.float32)
        values = rows[:, qwidth + kwidth:].reshape(group_rows, KVH, HD).astype(jnp.float32)
        keys = jnp.repeat(keys, shared, axis=1)
        values = jnp.repeat(values, shared, axis=1)
        scores = jnp.einsum('qhd,khd->hqk', query, keys) * HD ** (-0.5)
        places = jnp.arange(group_rows, dtype=jnp.int32)
        visible = (places[None, :] <= places[:, None]) & (places[None, :] >= first[:, None])
        scores = jnp.where(visible[None], scores, -1e+30)
        top = lax.optimization_barrier(jnp.max(scores, axis=-1, keepdims=True))
        weights = jnp.exp(scores - top)
        total = lax.optimization_barrier(jnp.sum(weights, axis=-1, keepdims=True))
        probs = lax.optimization_barrier(weights.astype(jnp.bfloat16)).astype(jnp.float32)
        numer = jnp.einsum('hqk,khd->qhd', probs, values)
        result = numer / jnp.transpose(total, (1, 0, 2))
        return result.astype(jnp.bfloat16).reshape(group_rows, qwidth)
    attn = lax.map(attend, (blocks, starts)).reshape(TOKENS, qwidth)
    share = QH // N_HEAD * HD
    summed = jnp.zeros((TOKENS, D), jnp.float32)
    for block in range(N_HEAD):
        part = jnp.dot(attn[:, block * share:(block + 1) * share], out_weight[block * share:(block + 1) * share], preferred_element_type=jnp.float32)
        summed = summed + lax.optimization_barrier(part.astype(jnp.bfloat16)).astype(jnp.float32)
    proj = summed.astype(jnp.bfloat16)
    arrived = proj[dest_row]
    new_residual = (residual.astype(jnp.float32) + arrived.astype(jnp.float32)).astype(jnp.bfloat16)
    stream = lax.optimization_barrier(new_residual).astype(jnp.float32)
    scale = lax.rsqrt(lax.optimization_barrier(jnp.mean(stream * stream, axis=-1, keepdims=True)) + 1e-06)
    normed = (stream * scale * norm_gain).astype(jnp.bfloat16)
    return (new_residual, normed)
```

```python
import functools

import jax
import jax.numpy as jnp
from jax import lax
from jax.experimental import pallas as pl
from jax.experimental.pallas import tpu as pltpu
from jax.sharding import Mesh
from jax.sharding import PartitionSpec as P

QH = 24
KVH = 4
HD = 128
LOG2E = 1.4426950408889634


def earlier_count(labels, order_keys):
    same = labels[:, None] == labels[None, :]
    before = order_keys[None, :] < order_keys[:, None]
    return jnp.sum((same & before).astype(jnp.int32), axis=1)


def attention_kernel(n_blocks, shared, hid_ref, q_ref, first_ref, *refs):
    kv_refs = refs[:n_blocks]
    out_ref, bias_ref = refs[n_blocks:]
    rows = q_ref.shape[0]
    kv_head = pl.program_id(0)
    h = hid_ref[0]

    @pl.when(kv_head == 0)
    def _():
        qplace = h * rows + lax.broadcasted_iota(jnp.int32, (rows, rows), 0)
        first = jnp.broadcast_to(first_ref[...], (rows, rows))
        within = lax.broadcasted_iota(jnp.int32, (rows, rows), 1)
        for s in range(n_blocks):
            kplace = lax.rem(h + n_blocks - s, n_blocks) * rows + within
            seen = (kplace <= qplace) & (kplace >= first)
            bias_ref[:, s * rows : (s + 1) * rows] = jnp.where(seen, 0.0, -1e30)

    keys = jnp.concatenate([ref[0] for ref in kv_refs], axis=0)
    values = jnp.concatenate([ref[1] for ref in kv_refs], axis=0)
    for i in range(shared):
        q = q_ref[:, i * HD : (i + 1) * HD]
        scores = lax.dot_general(
            q, keys, (((1,), (1,)), ((), ())), preferred_element_type=jnp.float32
        )
        scores = scores * (HD**-0.5 * LOG2E) + bias_ref[...]
        top = jnp.max(scores, axis=1, keepdims=True)
        weights = jnp.exp2(scores - top)
        total = jnp.sum(weights, axis=1, keepdims=True)
        numer = jnp.dot(
            weights.astype(jnp.bfloat16), values, preferred_element_type=jnp.float32
        )
        out_ref[:, i * HD : (i + 1) * HD] = (numer / total).astype(jnp.bfloat16)


def attention(hid, q, first, blocks):
    rows, n = q.shape[0], len(blocks)
    shared = QH // KVH
    grid_spec = pltpu.PrefetchScalarGridSpec(
        num_scalar_prefetch=1,
        grid=(KVH,),
        in_specs=[
            pl.BlockSpec((rows, shared * HD), lambda b, hid: (0, b)),
            pl.BlockSpec((rows, 1), lambda b, hid: (0, 0)),
        ]
        + [pl.BlockSpec((2, rows, HD), lambda b, hid: (0, 0, b))] * n,
        out_specs=pl.BlockSpec((rows, shared * HD), lambda b, hid: (0, b)),
        scratch_shapes=[pltpu.VMEM((rows, n * rows), jnp.float32)],
    )
    return pl.pallas_call(
        functools.partial(attention_kernel, n, shared),
        grid_spec=grid_spec,
        out_shape=jax.ShapeDtypeStruct((rows, QH * HD), jnp.bfloat16),
        compiler_params=pltpu.CompilerParams(dimension_semantics=("arbitrary",)),
    )(hid, q, first, *blocks)


def ring_blocks(x, axis, n, beside):
    right = [(i, (i + 1) % n) for i in range(n)]
    left = [(i, (i - 1) % n) for i in range(n)]
    blocks = [None] * n
    blocks[0] = x
    up = down = x
    for s in range(1, n // 2 + 1):
        up = lax.ppermute(up, axis, right)
        blocks[s] = up
        if s < n - n // 2:
            down = lax.ppermute(down, axis, left)
            blocks[n - s] = down
            up, down = lax.optimization_barrier((up, down))
        if s == n // 2 - 2:
            up, down, beside = lax.optimization_barrier((up, down, beside))
    return blocks, beside


def local(qkv, residual, dest_row, source_row, doc_start, out_weight, norm_gain):
    seq = ("y", "x", "core")
    n_seq = lax.axis_size(seq)
    n_head = lax.axis_size("z")
    core = lax.axis_index("core")
    h = lax.axis_index("z")
    tok_rows, full_width = qkv.shape
    capacity = max(2, 3 * tok_rows // (2 * n_seq))
    group_rows = tok_rows * n_head
    qwidth = QH * HD
    kwidth = KVH * HD
    width = out_weight.shape[1]
    half = width // 2

    def chunked(slots):
        return slots.reshape(n_seq, capacity * (slots.shape[1] // 128), 128)

    def exchange(chunks):
        got = lax.all_to_all(chunks, seq, split_axis=0, concat_axis=0, tiled=True)
        return got.reshape(n_seq * capacity, chunks.size // (n_seq * capacity))

    mine_w = lax.all_gather(
        lax.dynamic_slice(out_weight, (0, core * half), (out_weight.shape[0], half)),
        "z",
        axis=0,
        tiled=True,
    )

    slots_all = jnp.arange(n_seq * capacity, dtype=jnp.int32)
    target = dest_row // group_rows
    local_order = jnp.arange(tok_rows, dtype=jnp.int32)
    send_slot = target * capacity + earlier_count(target, local_order)
    sender = source_row // group_rows
    recv_slot = sender * capacity + earlier_count(sender, source_row)
    placing = (send_slot[None, :] == slots_all[:, None]).astype(jnp.bfloat16)
    picking = (recv_slot[:, None] == slots_all[None, :]).astype(jnp.bfloat16)
    returning = (recv_slot[None, :] == slots_all[:, None]).astype(jnp.bfloat16)
    restoring = (send_slot[:, None] == slots_all[None, :]).astype(jnp.bfloat16)

    def place(matrix, x):
        return jnp.dot(matrix, x, preferred_element_type=jnp.float32).astype(jnp.bfloat16)

    kv_rows = place(picking, exchange(chunked(place(placing, qkv[:, qwidth:]))))
    q_chunks = chunked(place(placing, qkv[:, :qwidth]))
    kv_rows, q_chunks = lax.optimization_barrier((kv_rows, q_chunks))
    q_rows = place(picking, exchange(q_chunks))
    kv_block = jnp.stack([kv_rows[:, :kwidth], kv_rows[:, kwidth:]])
    blocks, q_rows = ring_blocks(kv_block, "z", n_head, q_rows)
    mine_w, blocks[n_head // 2] = lax.optimization_barrier((mine_w, blocks[n_head // 2]))
    other_w = lax.ppermute(mine_w, "core", [(0, 1), (1, 0)])
    first = lax.dynamic_slice(doc_start, (h * tok_rows,), (tok_rows,))[:, None]
    attn = attention(h.astype(jnp.int32)[None], q_rows, first, blocks)

    ours = place(attn, mine_w)
    theirs = place(attn, other_w)
    proj = jnp.where(
        core == 0,
        jnp.concatenate([ours, theirs], axis=1),
        jnp.concatenate([theirs, ours], axis=1),
    )
    arrived = exchange(chunked(place(returning, proj)))
    mine = jnp.dot(restoring, arrived, preferred_element_type=jnp.float32)
    new_residual = (residual.astype(jnp.float32) + mine).astype(jnp.bfloat16)
    stream = lax.optimization_barrier(new_residual).astype(jnp.float32)
    factor = lax.rsqrt(jnp.mean(stream * stream, axis=-1, keepdims=True) + 1e-06)
    normed = (stream * factor * norm_gain).astype(jnp.bfloat16)
    return (new_residual, normed)


def solution(mesh):
    n_seq, n_head = mesh.devices.shape
    cores = 2
    xs = 4 if n_seq % 8 == 0 else 1
    fine = Mesh(
        mesh.devices.reshape(n_seq // (cores * xs), xs, cores, n_head), ("y", "x", "core", "z")
    )
    rows = ("y", "x", "core", "z")
    return jax.shard_map(
        local,
        mesh=fine,
        in_specs=(
            P(rows, None),
            P(rows, None),
            P(rows),
            P(rows),
            P(("y", "x", "core")),
            P("z", None),
            P(),
        ),
        out_specs=(P(rows, None), P(rows, None)),
        check_vma=False,
    )
```

```python
import functools

import jax
import jax.numpy as jnp
from jax import lax
from jax.experimental import pallas as pl
from jax.experimental.pallas import tpu as pltpu
from jax.sharding import Mesh
from jax.sharding import PartitionSpec as P

QH = 24
KVH = 4
HD = 128
LOG2E = 1.4426950408889634


def earlier_count(labels, order_keys):
    same = labels[:, None] == labels[None, :]
    before = order_keys[None, :] < order_keys[:, None]
    return jnp.sum((same & before).astype(jnp.int32), axis=1)


def attention_kernel(n_blocks, shared, hid_ref, q_ref, first_ref, *refs):
    kv_refs = refs[:n_blocks]
    out_ref, bias_ref = refs[n_blocks:]
    rows = q_ref.shape[0]
    kv_head = pl.program_id(0)
    h = hid_ref[0]

    @pl.when(kv_head == 0)
    def _():
        qplace = h * rows + lax.broadcasted_iota(jnp.int32, (rows, rows), 0)
        first = jnp.broadcast_to(first_ref[...], (rows, rows))
        within = lax.broadcasted_iota(jnp.int32, (rows, rows), 1)
        for s in range(n_blocks):
            kplace = lax.rem(h + n_blocks - s, n_blocks) * rows + within
            seen = (kplace <= qplace) & (kplace >= first)
            bias_ref[:, s * rows : (s + 1) * rows] = jnp.where(seen, 0.0, -1e30)

    keys = jnp.concatenate([ref[0] for ref in kv_refs], axis=0)
    values = jnp.concatenate([ref[1] for ref in kv_refs], axis=0)
    for i in range(shared):
        q = q_ref[:, i * HD : (i + 1) * HD]
        scores = lax.dot_general(
            q, keys, (((1,), (1,)), ((), ())), preferred_element_type=jnp.float32
        )
        scores = scores * (HD**-0.5 * LOG2E) + bias_ref[...]
        top = jnp.max(scores, axis=1, keepdims=True)
        weights = jnp.exp2(scores - top)
        total = jnp.sum(weights, axis=1, keepdims=True)
        numer = jnp.dot(
            weights.astype(jnp.bfloat16), values, preferred_element_type=jnp.float32
        )
        out_ref[:, i * HD : (i + 1) * HD] = (numer / total).astype(jnp.bfloat16)


def attention(hid, q, first, blocks):
    rows, n = q.shape[0], len(blocks)
    shared = QH // KVH
    grid_spec = pltpu.PrefetchScalarGridSpec(
        num_scalar_prefetch=1,
        grid=(KVH,),
        in_specs=[
            pl.BlockSpec((rows, shared * HD), lambda b, hid: (0, b)),
            pl.BlockSpec((rows, 1), lambda b, hid: (0, 0)),
        ]
        + [pl.BlockSpec((2, rows, HD), lambda b, hid: (0, 0, b))] * n,
        out_specs=pl.BlockSpec((rows, shared * HD), lambda b, hid: (0, b)),
        scratch_shapes=[pltpu.VMEM((rows, n * rows), jnp.float32)],
    )
    return pl.pallas_call(
        functools.partial(attention_kernel, n, shared),
        grid_spec=grid_spec,
        out_shape=jax.ShapeDtypeStruct((rows, QH * HD), jnp.bfloat16),
        compiler_params=pltpu.CompilerParams(dimension_semantics=("arbitrary",)),
    )(hid, q, first, *blocks)


def ring_blocks(x, axis, n, beside):
    right = [(i, (i + 1) % n) for i in range(n)]
    left = [(i, (i - 1) % n) for i in range(n)]
    blocks = [None] * n
    blocks[0] = x
    up = down = x
    for s in range(1, n // 2 + 1):
        up = lax.ppermute(up, axis, right)
        blocks[s] = up
        if s < n - n // 2:
            down = lax.ppermute(down, axis, left)
            blocks[n - s] = down
            up, down = lax.optimization_barrier((up, down))
        if s == n // 2 - 2:
            up, down, beside = lax.optimization_barrier((up, down, beside))
    return blocks, beside


def local(qkv, residual, dest_row, source_row, doc_start, out_weight, norm_gain):
    seq = ("y", "x", "core")
    n_seq = lax.axis_size(seq)
    n_head = lax.axis_size("z")
    core = lax.axis_index("core")
    h = lax.axis_index("z")
    tok_rows, full_width = qkv.shape
    capacity = max(2, 3 * tok_rows // (2 * n_seq))
    group_rows = tok_rows * n_head
    qwidth = QH * HD
    kwidth = KVH * HD
    width = out_weight.shape[1]

    def chunked(slots):
        return slots.reshape(n_seq, capacity * (slots.shape[1] // 128), 128)

    def exchange(chunks):
        got = lax.all_to_all(chunks, seq, split_axis=0, concat_axis=0, tiled=True)
        return got.reshape(n_seq * capacity, chunks.size // (n_seq * capacity))

    pieces = lax.axis_size("x") * lax.axis_size("core")
    piece = lax.axis_index("x") * lax.axis_size("core") + core
    share = out_weight.shape[0] // pieces
    weight = lax.all_gather(
        lax.dynamic_slice(out_weight, (piece * share, 0), (share, width)),
        ("z", "x", "core"),
        axis=0,
        tiled=True,
    )

    slots_all = jnp.arange(n_seq * capacity, dtype=jnp.int32)
    target = dest_row // group_rows
    local_order = jnp.arange(tok_rows, dtype=jnp.int32)
    send_slot = target * capacity + earlier_count(target, local_order)
    sender = source_row // group_rows
    recv_slot = sender * capacity + earlier_count(sender, source_row)
    placing = (send_slot[None, :] == slots_all[:, None]).astype(jnp.bfloat16)
    picking = (recv_slot[:, None] == slots_all[None, :]).astype(jnp.bfloat16)
    returning = (recv_slot[None, :] == slots_all[:, None]).astype(jnp.bfloat16)
    restoring = (send_slot[:, None] == slots_all[None, :]).astype(jnp.bfloat16)

    def place(matrix, x):
        return jnp.dot(matrix, x, preferred_element_type=jnp.float32).astype(jnp.bfloat16)

    kv_rows = place(picking, exchange(chunked(place(placing, qkv[:, qwidth:]))))
    q_chunks = chunked(place(placing, qkv[:, :qwidth]))
    kv_rows, q_chunks = lax.optimization_barrier((kv_rows, q_chunks))
    q_rows = place(picking, exchange(q_chunks))
    kv_block = jnp.stack([kv_rows[:, :kwidth], kv_rows[:, kwidth:]])
    blocks, q_rows = ring_blocks(kv_block, "z", n_head, q_rows)
    first = lax.dynamic_slice(doc_start, (h * tok_rows,), (tok_rows,))[:, None]
    attn = attention(h.astype(jnp.int32)[None], q_rows, first, blocks)

    proj = place(attn, weight)
    arrived = exchange(chunked(place(returning, proj)))
    mine = jnp.dot(restoring, arrived, preferred_element_type=jnp.float32)
    new_residual = (residual.astype(jnp.float32) + mine).astype(jnp.bfloat16)
    stream = lax.optimization_barrier(new_residual).astype(jnp.float32)
    factor = lax.rsqrt(jnp.mean(stream * stream, axis=-1, keepdims=True) + 1e-06)
    normed = (stream * factor * norm_gain).astype(jnp.bfloat16)
    return (new_residual, normed)


def solution(mesh):
    n_seq, n_head = mesh.devices.shape
    cores = 2
    xs = 4 if n_seq % 8 == 0 else 1
    fine = Mesh(
        mesh.devices.reshape(n_seq // (cores * xs), xs, cores, n_head), ("y", "x", "core", "z")
    )
    rows = ("y", "x", "core", "z")
    return jax.shard_map(
        local,
        mesh=fine,
        in_specs=(
            P(rows, None),
            P(rows, None),
            P(rows),
            P(rows),
            P(("y", "x", "core")),
            P("z", None),
            P(),
        ),
        out_specs=(P(rows, None), P(rows, None)),
        check_vma=False,
    )
```

```python
import functools

import jax
import jax.numpy as jnp
from jax import lax
from jax.experimental import pallas as pl
from jax.experimental.pallas import tpu as pltpu
from jax.sharding import Mesh
from jax.sharding import PartitionSpec as P

QH = 24
KVH = 4
HD = 128
LOG2E = 1.4426950408889634


def earlier_count(labels, order_keys):
    same = labels[:, None] == labels[None, :]
    before = order_keys[None, :] < order_keys[:, None]
    return jnp.sum((same & before).astype(jnp.int32), axis=1)


def attention_kernel(n_blocks, shared, hid_ref, q_ref, first_ref, *refs):
    kv_refs = refs[:n_blocks]
    out_ref, bias_ref = refs[n_blocks:]
    rows = q_ref.shape[0]
    kv_head = pl.program_id(0)
    h = hid_ref[0]
    turn = hid_ref[1]

    @pl.when(kv_head == 0)
    def _():
        qplace = h * rows + lax.broadcasted_iota(jnp.int32, (rows, rows), 0)
        first = jnp.broadcast_to(first_ref[...], (rows, rows))
        within = lax.broadcasted_iota(jnp.int32, (rows, rows), 1)
        for s in range(n_blocks):
            away = (s + 1) // 2 if s % 2 else -(s // 2)
            kplace = lax.rem(h + n_blocks - away * turn, n_blocks) * rows + within
            seen = (kplace <= qplace) & (kplace >= first)
            bias_ref[:, s * rows : (s + 1) * rows] = jnp.where(seen, 0.0, -1e30)

    keys = jnp.concatenate([ref[0] for ref in kv_refs], axis=0)
    values = jnp.concatenate([ref[1] for ref in kv_refs], axis=0)
    for i in range(shared):
        q = q_ref[:, i * HD : (i + 1) * HD]
        scores = lax.dot_general(
            q, keys, (((1,), (1,)), ((), ())), preferred_element_type=jnp.float32
        )
        scores = scores * (HD**-0.5 * LOG2E) + bias_ref[...]
        top = jnp.max(scores, axis=1, keepdims=True)
        weights = jnp.exp2(scores - top)
        total = jnp.sum(weights, axis=1, keepdims=True)
        numer = jnp.dot(
            weights.astype(jnp.bfloat16), values, preferred_element_type=jnp.float32
        )
        out_ref[:, i * HD : (i + 1) * HD] = (numer / total).astype(jnp.bfloat16)


def attention(hid, q, first, blocks):
    rows, n = q.shape[0], len(blocks)
    shared = QH // KVH
    grid_spec = pltpu.PrefetchScalarGridSpec(
        num_scalar_prefetch=1,
        grid=(KVH,),
        in_specs=[
            pl.BlockSpec((rows, shared * HD), lambda b, hid: (0, b)),
            pl.BlockSpec((rows, 1), lambda b, hid: (0, 0)),
        ]
        + [pl.BlockSpec((2, rows, HD), lambda b, hid: (0, 0, b))] * n,
        out_specs=pl.BlockSpec((rows, shared * HD), lambda b, hid: (0, b)),
        scratch_shapes=[pltpu.VMEM((rows, n * rows), jnp.float32)],
    )
    return pl.pallas_call(
        functools.partial(attention_kernel, n, shared),
        grid_spec=grid_spec,
        out_shape=jax.ShapeDtypeStruct((rows, QH * HD), jnp.bfloat16),
        compiler_params=pltpu.CompilerParams(dimension_semantics=("arbitrary",)),
    )(hid, q, first, *blocks)


def ring_blocks(x, n, beside):
    swap = [(0, 1), (1, 0)]
    ring = [(z, (z + 1) % n) for z in range(n)] + [(n + z, n + (z - 1) % n) for z in range(n)]
    width = x.shape[0]
    blocks = [x]
    load = jnp.concatenate([x, lax.ppermute(x, "core", swap)])
    for s in range(1, n // 2 + 1):
        held = load
        load = lax.ppermute(held[:width] if s == n // 2 else held, ("core", "z"), ring)
        if s > 1:
            other = lax.ppermute(held[width:], "core", swap)
            load, other = lax.optimization_barrier((load, other))
            blocks.append(other)
        blocks.append(load[:width])
        if s == n // 2 - 2:
            load, beside = lax.optimization_barrier((load, beside))
    return blocks, beside


def local(qkv, residual, dest_row, source_row, doc_start, out_weight, norm_gain):
    seq = ("y", "x", "core")
    n_seq = lax.axis_size(seq)
    n_head = lax.axis_size("z")
    core = lax.axis_index("core")
    h = lax.axis_index("z")
    tok_rows, full_width = qkv.shape
    capacity = max(2, 3 * tok_rows // (2 * n_seq))
    group_rows = tok_rows * n_head
    qwidth = QH * HD
    kwidth = KVH * HD
    width = out_weight.shape[1]

    def chunked(slots):
        return slots.reshape(n_seq, capacity * (slots.shape[1] // 128), 128)

    def exchange(chunks):
        got = lax.all_to_all(chunks, seq, split_axis=0, concat_axis=0, tiled=True)
        return got.reshape(n_seq * capacity, chunks.size // (n_seq * capacity))

    share = out_weight.shape[0] // lax.axis_size("core")
    weight = lax.all_gather(
        lax.dynamic_slice(out_weight, (core * share, 0), (share, width)),
        ("z", "core"),
        axis=0,
        tiled=True,
    )

    slots_all = jnp.arange(n_seq * capacity, dtype=jnp.int32)
    target = dest_row // group_rows
    local_order = jnp.arange(tok_rows, dtype=jnp.int32)
    send_slot = target * capacity + earlier_count(target, local_order)
    sender = source_row // group_rows
    recv_slot = sender * capacity + earlier_count(sender, source_row)
    placing = (send_slot[None, :] == slots_all[:, None]).astype(jnp.bfloat16)
    picking = (recv_slot[:, None] == slots_all[None, :]).astype(jnp.bfloat16)
    returning = (recv_slot[None, :] == slots_all[:, None]).astype(jnp.bfloat16)
    restoring = (send_slot[:, None] == slots_all[None, :]).astype(jnp.bfloat16)

    def place(matrix, x):
        return jnp.dot(matrix, x, preferred_element_type=jnp.float32).astype(jnp.bfloat16)

    kv_rows = place(picking, exchange(chunked(place(placing, qkv[:, qwidth:]))))
    q_chunks = chunked(place(placing, qkv[:, :qwidth]))
    kv_rows, q_chunks = lax.optimization_barrier((kv_rows, q_chunks))
    q_rows = place(picking, exchange(q_chunks))
    kv_block = jnp.stack([kv_rows[:, :kwidth], kv_rows[:, kwidth:]])
    blocks, q_rows = ring_blocks(kv_block, n_head, q_rows)
    first = lax.dynamic_slice(doc_start, (h * tok_rows,), (tok_rows,))[:, None]
    place_ids = jnp.stack([h, 1 - 2 * core]).astype(jnp.int32)
    attn = attention(place_ids, q_rows, first, blocks)

    proj = place(attn, weight)
    arrived = exchange(chunked(place(returning, proj)))
    mine = jnp.dot(restoring, arrived, preferred_element_type=jnp.float32)
    new_residual = (residual.astype(jnp.float32) + mine).astype(jnp.bfloat16)
    stream = lax.optimization_barrier(new_residual).astype(jnp.float32)
    factor = lax.rsqrt(jnp.mean(stream * stream, axis=-1, keepdims=True) + 1e-06)
    normed = (stream * factor * norm_gain).astype(jnp.bfloat16)
    return (new_residual, normed)


def solution(mesh):
    n_seq, n_head = mesh.devices.shape
    cores = 2
    xs = 4 if n_seq % 8 == 0 else 1
    fine = Mesh(
        mesh.devices.reshape(n_seq // (cores * xs), xs, cores, n_head), ("y", "x", "core", "z")
    )
    rows = ("y", "x", "core", "z")
    return jax.shard_map(
        local,
        mesh=fine,
        in_specs=(
            P(rows, None),
            P(rows, None),
            P(rows),
            P(rows),
            P(("y", "x", "core")),
            P("z", None),
            P(),
        ),
        out_specs=(P(rows, None), P(rows, None)),
        check_vma=False,
    )
```

```python
import functools

import jax
import jax.numpy as jnp
from jax import lax
from jax.experimental import pallas as pl
from jax.experimental.pallas import tpu as pltpu
from jax.sharding import Mesh
from jax.sharding import PartitionSpec as P

QH = 24
KVH = 4
HD = 128
LOG2E = 1.4426950408889634


def earlier_count(labels, order_keys):
    same = labels[:, None] == labels[None, :]
    before = order_keys[None, :] < order_keys[:, None]
    return jnp.sum((same & before).astype(jnp.int32), axis=1)


def attention_kernel(n_blocks, shared, hid_ref, q_ref, first_ref, *refs):
    kv_refs = refs[:n_blocks]
    out_ref, bias_ref = refs[n_blocks:]
    rows = q_ref.shape[0]
    kv_head = pl.program_id(0)
    h = hid_ref[0]

    @pl.when(kv_head == 0)
    def _():
        qplace = h * rows + lax.broadcasted_iota(jnp.int32, (rows, rows), 0)
        first = jnp.broadcast_to(first_ref[...], (rows, rows))
        within = lax.broadcasted_iota(jnp.int32, (rows, rows), 1)
        for s in range(n_blocks):
            kplace = lax.rem(h + n_blocks - s, n_blocks) * rows + within
            seen = (kplace <= qplace) & (kplace >= first)
            bias_ref[:, s * rows : (s + 1) * rows] = jnp.where(seen, 0.0, -1e30)

    keys = jnp.concatenate([ref[0] for ref in kv_refs], axis=0)
    values = jnp.concatenate([ref[1] for ref in kv_refs], axis=0)

    def scores_of(i):
        return lax.dot_general(
            q_ref[:, i * HD : (i + 1) * HD],
            keys,
            (((1,), (1,)), ((), ())),
            preferred_element_type=jnp.float32,
        )

    coming = scores_of(0)
    for i in range(shared):
        scores = coming
        if i + 1 < shared:
            coming = scores_of(i + 1)
        scores = scores * (HD**-0.5 * LOG2E) + bias_ref[...]
        top = jnp.max(scores, axis=1, keepdims=True)
        weights = jnp.exp2(scores - top)
        total = jnp.sum(weights, axis=1, keepdims=True)
        numer = jnp.dot(
            weights.astype(jnp.bfloat16), values, preferred_element_type=jnp.float32
        )
        out_ref[:, i * HD : (i + 1) * HD] = (numer / total).astype(jnp.bfloat16)


def attention(hid, q, first, blocks):
    rows, n = q.shape[0], len(blocks)
    shared = QH // KVH
    grid_spec = pltpu.PrefetchScalarGridSpec(
        num_scalar_prefetch=1,
        grid=(KVH,),
        in_specs=[
            pl.BlockSpec((rows, shared * HD), lambda b, hid: (0, b)),
            pl.BlockSpec((rows, 1), lambda b, hid: (0, 0)),
        ]
        + [pl.BlockSpec((2, rows, HD), lambda b, hid: (0, 0, b))] * n,
        out_specs=pl.BlockSpec((rows, shared * HD), lambda b, hid: (0, b)),
        scratch_shapes=[pltpu.VMEM((rows, n * rows), jnp.float32)],
    )
    return pl.pallas_call(
        functools.partial(attention_kernel, n, shared),
        grid_spec=grid_spec,
        out_shape=jax.ShapeDtypeStruct((rows, QH * HD), jnp.bfloat16),
        compiler_params=pltpu.CompilerParams(dimension_semantics=("arbitrary",)),
    )(hid, q, first, *blocks)


def project_kernel(attn_ref, strip_ref, placing_ref, out_ref):
    proj = jnp.dot(attn_ref[...], strip_ref[0], preferred_element_type=jnp.float32)
    out_ref[...] = jnp.dot(
        placing_ref[...], proj.astype(jnp.bfloat16), preferred_element_type=jnp.float32
    ).astype(jnp.bfloat16)


def project(attn, strips, placing):
    n, depth, share = strips.shape
    slots, rows = placing.shape
    return pl.pallas_call(
        project_kernel,
        grid=(n,),
        in_specs=[
            pl.BlockSpec((rows, depth), lambda j: (0, 0)),
            pl.BlockSpec((1, depth, share), lambda j: (j, 0, 0)),
            pl.BlockSpec((slots, rows), lambda j: (0, 0)),
        ],
        out_specs=pl.BlockSpec((slots, share), lambda j: (0, j)),
        out_shape=jax.ShapeDtypeStruct((slots, n * share), jnp.bfloat16),
        compiler_params=pltpu.CompilerParams(dimension_semantics=("arbitrary",)),
    )(attn, strips, placing)


def ring_blocks(x, axis, n, due):
    right = [(i, (i + 1) % n) for i in range(n)]
    left = [(i, (i - 1) % n) for i in range(n)]
    blocks = [None] * n
    blocks[0] = x
    up = down = x
    for s in range(1, n // 2 + 1):
        up = lax.ppermute(up, axis, right)
        blocks[s] = up
        if s < n - n // 2:
            down = lax.ppermute(down, axis, left)
            blocks[n - s] = down
            up, down = lax.optimization_barrier((up, down))
        if s in due:
            up, down, due[s] = lax.optimization_barrier((up, down, due[s]))
    return blocks, due


def local(qkv, residual, dest_row, source_row, doc_start, out_weight, norm_gain):
    seq = ("y", "x", "core")
    n_seq = lax.axis_size(seq)
    n_head = lax.axis_size("z")
    core = lax.axis_index("core")
    h = lax.axis_index("z")
    tok_rows, _ = qkv.shape
    capacity = max(2, 3 * tok_rows // (2 * n_seq))
    group_rows = tok_rows * n_head
    qwidth = QH * HD
    kwidth = KVH * HD
    width = out_weight.shape[1]

    def chunked(slots):
        return slots.reshape(n_seq, capacity * (slots.shape[1] // 128), 128)

    def exchange(chunks):
        got = lax.all_to_all(chunks, seq, split_axis=0, concat_axis=0, tiled=True)
        return got.reshape(n_seq * capacity, chunks.size // (n_seq * capacity))

    pieces = lax.axis_size("x") * lax.axis_size("core")
    piece = lax.axis_index("x") * lax.axis_size("core") + core
    share = width // pieces
    strip = lax.all_gather(
        lax.dynamic_slice(out_weight, (0, piece * share), (out_weight.shape[0], share)),
        "z",
        axis=0,
        tiled=True,
    )

    slots_all = jnp.arange(n_seq * capacity, dtype=jnp.int32)
    target = dest_row // group_rows
    local_order = jnp.arange(tok_rows, dtype=jnp.int32)
    send_slot = target * capacity + earlier_count(target, local_order)
    sender = source_row // group_rows
    recv_slot = sender * capacity + earlier_count(sender, source_row)
    placing = (send_slot[None, :] == slots_all[:, None]).astype(jnp.bfloat16)
    picking = (recv_slot[:, None] == slots_all[None, :]).astype(jnp.bfloat16)
    returning = (recv_slot[None, :] == slots_all[:, None]).astype(jnp.bfloat16)
    restoring = (send_slot[:, None] == slots_all[None, :]).astype(jnp.bfloat16)

    def place(matrix, x):
        return jnp.dot(matrix, x, preferred_element_type=jnp.float32).astype(jnp.bfloat16)

    kv_rows = place(picking, exchange(chunked(place(placing, qkv[:, qwidth:]))))
    q_chunks = chunked(place(placing, qkv[:, :qwidth]))
    kv_rows, q_chunks = lax.optimization_barrier((kv_rows, q_chunks))
    q_arrived = exchange(q_chunks)
    q_rows = place(picking, q_arrived)
    kv_block = jnp.stack([kv_rows[:, :kwidth], kv_rows[:, kwidth:]])
    blocks, due = ring_blocks(kv_block, "z", n_head, {2: strip, n_head // 2 - 2: q_rows})
    q_rows = due[n_head // 2 - 2]
    strips = lax.all_gather(due[2], ("x", "core"), axis=0)
    first = lax.dynamic_slice(doc_start, (h * tok_rows,), (tok_rows,))[:, None]
    attn = attention(h.astype(jnp.int32)[None], q_rows, first, blocks)

    arrived = exchange(chunked(project(attn, strips, returning)))
    mine = jnp.dot(restoring, arrived, preferred_element_type=jnp.float32)
    new_residual = (residual.astype(jnp.float32) + mine).astype(jnp.bfloat16)
    stream = lax.optimization_barrier(new_residual).astype(jnp.float32)
    factor = lax.rsqrt(jnp.mean(stream * stream, axis=-1, keepdims=True) + 1e-06)
    normed = (stream * factor * norm_gain).astype(jnp.bfloat16)
    return (new_residual, normed)


def solution(mesh):
    n_seq, n_head = mesh.devices.shape
    cores = 2
    xs = 4 if n_seq % 8 == 0 else 1
    fine = Mesh(
        mesh.devices.reshape(n_seq // (cores * xs), xs, cores, n_head), ("y", "x", "core", "z")
    )
    rows = ("y", "x", "core", "z")

    return jax.shard_map(
        local,
        mesh=fine,
        in_specs=(
            P(rows, None),
            P(rows, None),
            P(rows),
            P(rows),
            P(("y", "x", "core")),
            P("z", None),
            P(),
        ),
        out_specs=(P(rows, None), P(rows, None)),
        check_vma=False,
    )
```

```python
import functools

import jax
import jax.numpy as jnp
from jax import lax
from jax.experimental import pallas as pl
from jax.experimental.pallas import tpu as pltpu
from jax.sharding import Mesh
from jax.sharding import PartitionSpec as P

QH = 24
KVH = 4
HD = 128
LOG2E = 1.4426950408889634


def earlier_count(labels, order_keys):
    same = labels[:, None] == labels[None, :]
    before = order_keys[None, :] < order_keys[:, None]
    return jnp.sum((same & before).astype(jnp.int32), axis=1)


def fill_bias(bias_ref, first_ref, h, blocks_below, n_ring):
    rows = bias_ref.shape[0]
    qplace = h * rows + lax.broadcasted_iota(jnp.int32, (rows, rows), 0)
    first = jnp.broadcast_to(first_ref[...], (rows, rows))
    within = lax.broadcasted_iota(jnp.int32, (rows, rows), 1)
    for i, below in enumerate(blocks_below):
        kplace = lax.rem(h + n_ring - below, n_ring) * rows + within
        seen = (kplace <= qplace) & (kplace >= first)
        bias_ref[:, i * rows : (i + 1) * rows] = jnp.where(seen, 0.0, -1e30)


def scores_of(q_ref, i, keys):
    return lax.dot_general(
        q_ref[:, i * HD : (i + 1) * HD],
        keys,
        (((1,), (1,)), ((), ())),
        preferred_element_type=jnp.float32,
    )


def early_kernel(below, n_ring, shared, hid_ref, q_ref, first_ref, *refs):
    kv_refs = refs[: len(below)]
    numer_ref, top_ref, total_ref, bias_ref = refs[len(below) :]

    @pl.when(pl.program_id(0) == 0)
    def _():
        fill_bias(bias_ref, first_ref, hid_ref[0], below, n_ring)

    keys = jnp.concatenate([ref[0] for ref in kv_refs], axis=0)
    values = jnp.concatenate([ref[1] for ref in kv_refs], axis=0)
    lane = lax.broadcasted_iota(jnp.int32, top_ref.shape[1:], 1)
    tops = jnp.zeros(top_ref.shape[1:], jnp.float32)
    totals = jnp.zeros(top_ref.shape[1:], jnp.float32)
    coming = scores_of(q_ref, 0, keys)
    for i in range(shared):
        scores = coming
        if i + 1 < shared:
            coming = scores_of(q_ref, i + 1, keys)
        scores = scores * (HD**-0.5 * LOG2E) + bias_ref[...]
        top = jnp.max(scores, axis=1, keepdims=True)
        weights = jnp.exp2(scores - top)
        tops = jnp.where(lane == i, top, tops)
        totals = jnp.where(lane == i, jnp.sum(weights, axis=1, keepdims=True), totals)
        numer_ref[:, i * HD : (i + 1) * HD] = jnp.dot(
            weights.astype(jnp.bfloat16), values, preferred_element_type=jnp.float32
        )
    top_ref[0] = tops
    total_ref[0] = totals


def late_kernel(below, n_ring, shared, hid_ref, q_ref, first_ref, kv_ref, numer_ref, top_ref, total_ref, out_ref, bias_ref):
    @pl.when(pl.program_id(0) == 0)
    def _():
        fill_bias(bias_ref, first_ref, hid_ref[0], (below,), n_ring)

    for i in range(shared):
        scores = scores_of(q_ref, i, kv_ref[0]) * (HD**-0.5 * LOG2E) + bias_ref[...]
        before = top_ref[0][:, i : i + 1]
        top = jnp.maximum(before, jnp.max(scores, axis=1, keepdims=True))
        weights = jnp.exp2(scores - top)
        keep = jnp.exp2(before - top)
        total = total_ref[0][:, i : i + 1] * keep + jnp.sum(weights, axis=1, keepdims=True)
        numer = numer_ref[:, i * HD : (i + 1) * HD] * keep + jnp.dot(
            weights.astype(jnp.bfloat16), kv_ref[1], preferred_element_type=jnp.float32
        )
        out_ref[:, i * HD : (i + 1) * HD] = (numer / total).astype(jnp.bfloat16)


def attention(hid, q, first, blocks):
    rows, n = q.shape[0], len(blocks)
    shared = QH // KVH
    last = n // 2
    below = [s for s in range(n) if s != last]
    wide = pl.BlockSpec((rows, shared * HD), lambda b, hid: (0, b))
    column = pl.BlockSpec((rows, 1), lambda b, hid: (0, 0))
    pair = pl.BlockSpec((2, rows, HD), lambda b, hid: (0, 0, b))
    stat = pl.BlockSpec((1, rows, HD), lambda b, hid: (b, 0, 0))
    stat_shape = jax.ShapeDtypeStruct((KVH, rows, HD), jnp.float32)
    params = pltpu.CompilerParams(dimension_semantics=("arbitrary",))
    numer, top, total = pl.pallas_call(
        functools.partial(early_kernel, below, n, shared),
        grid_spec=pltpu.PrefetchScalarGridSpec(
            num_scalar_prefetch=1,
            grid=(KVH,),
            in_specs=[wide, column] + [pair] * len(below),
            out_specs=[wide, stat, stat],
            scratch_shapes=[pltpu.VMEM((rows, len(below) * rows), jnp.float32)],
        ),
        out_shape=[jax.ShapeDtypeStruct(q.shape, jnp.float32), stat_shape, stat_shape],
        compiler_params=params,
    )(hid, q, first, *[blocks[s] for s in below])
    return pl.pallas_call(
        functools.partial(late_kernel, last, n, shared),
        grid_spec=pltpu.PrefetchScalarGridSpec(
            num_scalar_prefetch=1,
            grid=(KVH,),
            in_specs=[wide, column, pair, wide, stat, stat],
            out_specs=wide,
            scratch_shapes=[pltpu.VMEM((rows, rows), jnp.float32)],
        ),
        out_shape=jax.ShapeDtypeStruct(q.shape, jnp.bfloat16),
        compiler_params=params,
    )(hid, q, first, blocks[last], numer, top, total)


def ring_blocks(x, axis, n, beside):
    right = [(i, (i + 1) % n) for i in range(n)]
    left = [(i, (i - 1) % n) for i in range(n)]
    blocks = [None] * n
    blocks[0] = x
    up = down = x
    for s in range(1, n // 2 + 1):
        up = lax.ppermute(up, axis, right)
        blocks[s] = up
        if s < n - n // 2:
            down = lax.ppermute(down, axis, left)
            blocks[n - s] = down
            up, down = lax.optimization_barrier((up, down))
        if s == n // 2 - 2:
            up, down, beside = lax.optimization_barrier((up, down, beside))
    return blocks, beside


def local(qkv, residual, dest_row, source_row, doc_start, out_weight, norm_gain):
    seq = ("y", "x", "core")
    n_seq = lax.axis_size(seq)
    n_head = lax.axis_size("z")
    core = lax.axis_index("core")
    h = lax.axis_index("z")
    tok_rows, full_width = qkv.shape
    capacity = max(2, 3 * tok_rows // (2 * n_seq))
    group_rows = tok_rows * n_head
    qwidth = QH * HD
    kwidth = KVH * HD
    width = out_weight.shape[1]

    def chunked(slots):
        return slots.reshape(n_seq, capacity * (slots.shape[1] // 128), 128)

    def exchange(chunks):
        got = lax.all_to_all(chunks, seq, split_axis=0, concat_axis=0, tiled=True)
        return got.reshape(n_seq * capacity, chunks.size // (n_seq * capacity))

    pieces = lax.axis_size("x") * lax.axis_size("core")
    piece = lax.axis_index("x") * lax.axis_size("core") + core
    share = out_weight.shape[0] // pieces
    weight = lax.all_gather(
        lax.dynamic_slice(out_weight, (piece * share, 0), (share, width)),
        ("z", "x", "core"),
        axis=0,
        tiled=True,
    )

    slots_all = jnp.arange(n_seq * capacity, dtype=jnp.int32)
    target = dest_row // group_rows
    local_order = jnp.arange(tok_rows, dtype=jnp.int32)
    send_slot = target * capacity + earlier_count(target, local_order)
    sender = source_row // group_rows
    recv_slot = sender * capacity + earlier_count(sender, source_row)
    placing = (send_slot[None, :] == slots_all[:, None]).astype(jnp.bfloat16)
    picking = (recv_slot[:, None] == slots_all[None, :]).astype(jnp.bfloat16)
    returning = (recv_slot[None, :] == slots_all[:, None]).astype(jnp.bfloat16)
    restoring = (send_slot[:, None] == slots_all[None, :]).astype(jnp.bfloat16)

    def place(matrix, x):
        return jnp.dot(matrix, x, preferred_element_type=jnp.float32).astype(jnp.bfloat16)

    kv_rows = place(picking, exchange(chunked(place(placing, qkv[:, qwidth:]))))
    q_chunks = chunked(place(placing, qkv[:, :qwidth]))
    kv_rows, q_chunks = lax.optimization_barrier((kv_rows, q_chunks))
    q_rows = place(picking, exchange(q_chunks))
    kv_block = jnp.stack([kv_rows[:, :kwidth], kv_rows[:, kwidth:]])
    blocks, q_rows = ring_blocks(kv_block, "z", n_head, q_rows)
    first = lax.dynamic_slice(doc_start, (h * tok_rows,), (tok_rows,))[:, None]
    attn = attention(h.astype(jnp.int32)[None], q_rows, first, blocks)

    proj = place(attn, weight)
    arrived = exchange(chunked(place(returning, proj)))
    mine = jnp.dot(restoring, arrived, preferred_element_type=jnp.float32)
    new_residual = (residual.astype(jnp.float32) + mine).astype(jnp.bfloat16)
    stream = lax.optimization_barrier(new_residual).astype(jnp.float32)
    factor = lax.rsqrt(jnp.mean(stream * stream, axis=-1, keepdims=True) + 1e-06)
    normed = (stream * factor * norm_gain).astype(jnp.bfloat16)
    return (new_residual, normed)


def solution(mesh):
    n_seq, n_head = mesh.devices.shape
    cores = 2
    xs = 4 if n_seq % 8 == 0 else 1
    fine = Mesh(
        mesh.devices.reshape(n_seq // (cores * xs), xs, cores, n_head), ("y", "x", "core", "z")
    )
    rows = ("y", "x", "core", "z")
    return jax.shard_map(
        local,
        mesh=fine,
        in_specs=(
            P(rows, None),
            P(rows, None),
            P(rows),
            P(rows),
            P(("y", "x", "core")),
            P("z", None),
            P(),
        ),
        out_specs=(P(rows, None), P(rows, None)),
        check_vma=False,
    )
```

```python
import functools

import jax
import jax.numpy as jnp
from jax import lax
from jax.experimental import pallas as pl
from jax.experimental.pallas import tpu as pltpu
from jax.sharding import Mesh
from jax.sharding import PartitionSpec as P

QH = 24
KVH = 4
HD = 128
LOG2E = 1.4426950408889634


def earlier_count(labels, order_keys):
    same = labels[:, None] == labels[None, :]
    before = order_keys[None, :] < order_keys[:, None]
    return jnp.sum((same & before).astype(jnp.int32), axis=1)


def fill_bias(bias_ref, first_ref, h, blocks_below, n_ring):
    rows = bias_ref.shape[0]
    qplace = h * rows + lax.broadcasted_iota(jnp.int32, (rows, rows), 0)
    first = jnp.broadcast_to(first_ref[...], (rows, rows))
    within = lax.broadcasted_iota(jnp.int32, (rows, rows), 1)
    for i, below in enumerate(blocks_below):
        kplace = lax.rem(h + n_ring - below, n_ring) * rows + within
        seen = (kplace <= qplace) & (kplace >= first)
        bias_ref[:, i * rows : (i + 1) * rows] = jnp.where(seen, 0.0, -1e30)


def scores_of(q_ref, i, keys):
    return lax.dot_general(
        q_ref[:, i * HD : (i + 1) * HD],
        keys,
        (((1,), (1,)), ((), ())),
        preferred_element_type=jnp.float32,
    )


def early_kernel(below, n_ring, shared, hid_ref, q_ref, first_ref, *refs):
    kv_refs = refs[: len(below)]
    numer_ref, top_ref, total_ref, bias_ref = refs[len(below) :]

    @pl.when(pl.program_id(0) == 0)
    def _():
        fill_bias(bias_ref, first_ref, hid_ref[0], below, n_ring)

    keys = jnp.concatenate([ref[0] for ref in kv_refs], axis=0)
    values = jnp.concatenate([ref[1] for ref in kv_refs], axis=0)
    lane = lax.broadcasted_iota(jnp.int32, top_ref.shape[1:], 1)
    tops = jnp.zeros(top_ref.shape[1:], jnp.float32)
    totals = jnp.zeros(top_ref.shape[1:], jnp.float32)
    coming = scores_of(q_ref, 0, keys)
    for i in range(shared):
        scores = coming
        if i + 1 < shared:
            coming = scores_of(q_ref, i + 1, keys)
        scores = scores * (HD**-0.5 * LOG2E) + bias_ref[...]
        top = jnp.max(scores, axis=1, keepdims=True)
        weights = jnp.exp2(scores - top)
        tops = jnp.where(lane == i, top, tops)
        totals = jnp.where(lane == i, jnp.sum(weights, axis=1, keepdims=True), totals)
        numer_ref[:, i * HD : (i + 1) * HD] = jnp.dot(
            weights.astype(jnp.bfloat16), values, preferred_element_type=jnp.float32
        )
    top_ref[0] = tops
    total_ref[0] = totals


def late_kernel(below, n_ring, shared, hid_ref, q_ref, first_ref, kv_ref, numer_ref, top_ref, total_ref, out_ref, bias_ref):
    @pl.when(pl.program_id(0) == 0)
    def _():
        fill_bias(bias_ref, first_ref, hid_ref[0], (below,), n_ring)

    heads = range(shared)
    part = [slice(i * HD, (i + 1) * HD) for i in heads]
    before = [jnp.broadcast_to(top_ref[0][:, i : i + 1], bias_ref.shape) for i in heads]
    raw = [scores_of(q_ref, i, kv_ref[0]) for i in heads]
    scores = [raw[i] * (HD**-0.5 * LOG2E) + bias_ref[...] for i in heads]
    top = [jnp.maximum(before[i], jnp.max(scores[i], axis=1, keepdims=True)) for i in heads]
    weights = [jnp.exp2(scores[i] - top[i]) for i in heads]
    keep = [jnp.exp2(before[i] - top[i]) for i in heads]
    late = [
        jnp.dot(weights[i].astype(jnp.bfloat16), kv_ref[1], preferred_element_type=jnp.float32)
        for i in heads
    ]
    sums = [jnp.sum(weights[i], axis=1, keepdims=True) for i in heads]
    for i in heads:
        total = total_ref[0][:, i : i + 1] * keep[i] + sums[i]
        out_ref[:, part[i]] = (
            (numer_ref[:, part[i]] * keep[i] + late[i]) / total
        ).astype(jnp.bfloat16)


def attention(hid, q, first, blocks):
    rows, n = q.shape[0], len(blocks)
    shared = QH // KVH
    last = n // 2
    below = [s for s in range(n) if s != last]
    wide = pl.BlockSpec((rows, shared * HD), lambda b, hid: (0, b))
    column = pl.BlockSpec((rows, 1), lambda b, hid: (0, 0))
    pair = pl.BlockSpec((2, rows, HD), lambda b, hid: (0, 0, b))
    stat = pl.BlockSpec((1, rows, HD), lambda b, hid: (b, 0, 0))
    stat_shape = jax.ShapeDtypeStruct((KVH, rows, HD), jnp.float32)
    params = pltpu.CompilerParams(dimension_semantics=("arbitrary",))
    numer, top, total = pl.pallas_call(
        functools.partial(early_kernel, below, n, shared),
        grid_spec=pltpu.PrefetchScalarGridSpec(
            num_scalar_prefetch=1,
            grid=(KVH,),
            in_specs=[wide, column] + [pair] * len(below),
            out_specs=[wide, stat, stat],
            scratch_shapes=[pltpu.VMEM((rows, len(below) * rows), jnp.float32)],
        ),
        out_shape=[jax.ShapeDtypeStruct(q.shape, jnp.float32), stat_shape, stat_shape],
        compiler_params=params,
    )(hid, q, first, *[blocks[s] for s in below])
    return pl.pallas_call(
        functools.partial(late_kernel, last, n, shared),
        grid_spec=pltpu.PrefetchScalarGridSpec(
            num_scalar_prefetch=1,
            grid=(KVH,),
            in_specs=[wide, column, pair, wide, stat, stat],
            out_specs=wide,
            scratch_shapes=[pltpu.VMEM((rows, rows), jnp.float32)],
        ),
        out_shape=jax.ShapeDtypeStruct(q.shape, jnp.bfloat16),
        compiler_params=params,
    )(hid, q, first, blocks[last], numer, top, total)


def ring_blocks(x, axis, n, beside):
    right = [(i, (i + 1) % n) for i in range(n)]
    left = [(i, (i - 1) % n) for i in range(n)]
    blocks = [None] * n
    blocks[0] = x
    up = down = x
    for s in range(1, n // 2 + 1):
        up = lax.ppermute(up, axis, right)
        blocks[s] = up
        if s < n - n // 2:
            down = lax.ppermute(down, axis, left)
            blocks[n - s] = down
            up, down = lax.optimization_barrier((up, down))
        if s == n // 2 - 2:
            up, down, beside = lax.optimization_barrier((up, down, beside))
    return blocks, beside


def local(qkv, residual, dest_row, source_row, doc_start, out_weight, norm_gain):
    seq = ("y", "x", "core")
    n_seq = lax.axis_size(seq)
    n_head = lax.axis_size("z")
    core = lax.axis_index("core")
    h = lax.axis_index("z")
    tok_rows, full_width = qkv.shape
    capacity = max(2, 3 * tok_rows // (2 * n_seq))
    group_rows = tok_rows * n_head
    qwidth = QH * HD
    kwidth = KVH * HD
    width = out_weight.shape[1]

    def chunked(slots):
        return slots.reshape(n_seq, capacity * (slots.shape[1] // 128), 128)

    def exchange(chunks):
        got = lax.all_to_all(chunks, seq, split_axis=0, concat_axis=0, tiled=True)
        return got.reshape(n_seq * capacity, chunks.size // (n_seq * capacity))

    pieces = lax.axis_size("x") * lax.axis_size("core")
    piece = lax.axis_index("x") * lax.axis_size("core") + core
    share = out_weight.shape[0] // pieces
    weight = lax.all_gather(
        lax.dynamic_slice(out_weight, (piece * share, 0), (share, width)),
        ("z", "x", "core"),
        axis=0,
        tiled=True,
    )

    slots_all = jnp.arange(n_seq * capacity, dtype=jnp.int32)
    target = dest_row // group_rows
    local_order = jnp.arange(tok_rows, dtype=jnp.int32)
    send_slot = target * capacity + earlier_count(target, local_order)
    sender = source_row // group_rows
    recv_slot = sender * capacity + earlier_count(sender, source_row)
    placing = (send_slot[None, :] == slots_all[:, None]).astype(jnp.bfloat16)
    picking = (recv_slot[:, None] == slots_all[None, :]).astype(jnp.bfloat16)
    returning = (recv_slot[None, :] == slots_all[:, None]).astype(jnp.bfloat16)
    restoring = (send_slot[:, None] == slots_all[None, :]).astype(jnp.bfloat16)

    def place(matrix, x):
        return jnp.dot(matrix, x, preferred_element_type=jnp.float32).astype(jnp.bfloat16)

    kv_rows = place(picking, exchange(chunked(place(placing, qkv[:, qwidth:]))))
    q_chunks = chunked(place(placing, qkv[:, :qwidth]))
    kv_rows, q_chunks = lax.optimization_barrier((kv_rows, q_chunks))
    q_rows = place(picking, exchange(q_chunks))
    kv_block = jnp.stack([kv_rows[:, :kwidth], kv_rows[:, kwidth:]])
    blocks, q_rows = ring_blocks(kv_block, "z", n_head, q_rows)
    first = lax.dynamic_slice(doc_start, (h * tok_rows,), (tok_rows,))[:, None]
    attn = attention(h.astype(jnp.int32)[None], q_rows, first, blocks)

    proj = place(attn, weight)
    arrived = exchange(chunked(place(returning, proj)))
    mine = jnp.dot(restoring, arrived, preferred_element_type=jnp.float32)
    new_residual = (residual.astype(jnp.float32) + mine).astype(jnp.bfloat16)
    stream = lax.optimization_barrier(new_residual).astype(jnp.float32)
    factor = lax.rsqrt(jnp.mean(stream * stream, axis=-1, keepdims=True) + 1e-06)
    normed = (stream * factor * norm_gain).astype(jnp.bfloat16)
    return (new_residual, normed)


def solution(mesh):
    n_seq, n_head = mesh.devices.shape
    cores = 2
    xs = 4 if n_seq % 8 == 0 else 1
    fine = Mesh(
        mesh.devices.reshape(n_seq // (cores * xs), xs, cores, n_head), ("y", "x", "core", "z")
    )
    rows = ("y", "x", "core", "z")
    return jax.shard_map(
        local,
        mesh=fine,
        in_specs=(
            P(rows, None),
            P(rows, None),
            P(rows),
            P(rows),
            P(("y", "x", "core")),
            P("z", None),
            P(),
        ),
        out_specs=(P(rows, None), P(rows, None)),
        check_vma=False,
    )
```
